256 devices in a mesh: seq: 64 (over x, z, core), head: 4 (over y).
Axes of the slice: x: 4, y: 4, z: 8, core: 2. Of those that a mesh axis runs over, the one named last changes fastest.
Arguments:
- values: float32 [16384, 2560], P('seq', 'head'), may hold values from -6 to 6
- input_map: float32 [16384, 128], P('seq'), may hold values from -6 to 6
- output_map: float32 [16384, 128], P('seq'), may hold values from -6 to 6
- step_sizes: float32 [40, 16384], P('head', 'seq'), may hold values from 0.004 to 0.02
- decay_rates: float32 [40], P('head'), may hold values from 0.02 to 2
- skip_gains: float32 [40], P('head'), may hold values from 0.5 to 1.5
- doc_lengths: int32 [128], replicated, may hold values from 1 to 1024, 16384 in all
- out_grad: float32 [16384, 2560], P('seq', 'head'), may hold values from -6 to 6
Outputs:
- outputs: bfloat16 [16384, 2560], P('seq', 'head')
- grad_values: bfloat16 [16384, 2560], P('seq', 'head')
- grad_input_map: float32 [16384, 128], P('seq')
- grad_output_map: float32 [16384, 128], P('seq')
The draws below stay inside these ranges and needn't reach their ends.
Inputs may be any that keep to these rules, and one draw needn't show every extreme that they name: `doc_lengths`: the documents fill the stream of 16384 tokens in order; no document has more than 1024 tokens, and one has exactly that many.
All inputs are finite; a program needn't handle non-finite values.
Results may differ from the reference program's by a relative error of at most 0.001.
Values sent between devices are 32-bit elements; how exact they have to be, the bound alone decides.
No kernel may reach another device: no remote copies, remote signals or barrier semaphores. Data moves between devices by JAX's collectives and lax.ppermute only.
A program may use at most 128 MiB of HBM per device.

```python
import math
import jax
import jax.numpy as jnp
import numpy as np
from jax import lax

HEAD_SIZE = 64
STATE = 128
HEADS = 40
GROUP = 256
DOC_SPAN = 4
TOK_DEV = 256
TOKENS = 16384
NDOCS = 128


def shard_levels(own_key, dims, cuts, low, high):
    loudness = 1.0
    for axis_at, parts in cuts:
        steps = jax.random.uniform(jax.random.fold_in(jax.random.fold_in(own_key, 6), axis_at), (parts,), jnp.float32, low / len(cuts), high / len(cuts))
        loudness = loudness * jnp.repeat(jnp.exp(steps), dims[axis_at] // parts).reshape((-1,) + (1,) * (len(dims) - 1 - axis_at))
    return loudness


def split_up(count, total, reach, slope):
    portions = [(1 << 20) // math.isqrt(rank ** slope) + 1 for rank in range(2, count + 1)]
    spare, counts = total - reach - (count - 1), [1] * (count - 1)
    while spare > 0:
        movable = [i for i in range(count - 1) if counts[i] < reach]
        mass, remaining = sum([portions[i] for i in movable]), spare
        for i in movable:
            more = min(reach - counts[i], max(1, remaining * portions[i] // mass), spare)
            counts[i] = counts[i] + more
            spare = spare - more
    return np.array([reach] + counts)


def ragged_sizes(stream_key, number_of, total, limit, skew):
    if number_of == 2:
        one = jax.random.randint(stream_key, (), max(1, total - limit), min(limit, total - 1) + 1)
        return jnp.stack([one, total - one])
    sizes = jnp.asarray(split_up(number_of, total, limit, skew), jnp.int32)
    pairs = (number_of - 1) // 2
    source_of, receiver = sizes[1:1 + 2 * pairs:2], sizes[2:2 + 2 * pairs:2]
    room = jnp.minimum(source_of - 1, limit - receiver)
    passed = jax.random.randint(jax.random.fold_in(stream_key, 1), (pairs,), 0, 1 << 20) % (room + 1)
    sizes = sizes.at[1:1 + 2 * pairs:2].set(source_of - passed).at[2:2 + 2 * pairs:2].set(receiver + passed)
    return sizes[jax.random.permutation(jax.random.fold_in(stream_key, 2), number_of)]


def centred(key, extent, deviation, reach, shards=(), held_as=jnp.bfloat16):
    values = jax.random.normal(key, extent, jnp.float32) * deviation
    if len(shards) > 0:
        values = shard_levels(key, extent, shards, -0.22, 0.18) * values
    return jnp.clip(values, min=-reach, max=reach).astype(held_as)


def setup_inputs(seed: int = 0) -> dict:
    arg_keys = jax.random.split(jax.random.key(seed), 9)
    values = centred(arg_keys[0], (TOKENS, HEADS * HEAD_SIZE), 1.0, 6.0, ((0, 64), (1, 4)), jnp.float32)
    input_map = centred(arg_keys[1], (TOKENS, STATE), 1.0, 6.0, ((0, 64),), jnp.float32)
    output_map = centred(arg_keys[2], (TOKENS, STATE), 1.0, 6.0, ((0, 64),), jnp.float32)
    step_sizes = jnp.clip(jnp.exp(math.log(0.02) - 1.6094378 * jax.random.uniform(arg_keys[3], (HEADS, TOKENS), jnp.float32) ** shard_levels(arg_keys[3], (HEADS, TOKENS), ((0, 4), (1, 64)), -0.2, 0.2)), 0.004, 0.02)
    decay_rates = jnp.clip(jnp.exp(math.log(2.0) - 4.6051702 * jax.random.uniform(arg_keys[4], (HEADS,), jnp.float32) ** shard_levels(arg_keys[4], (HEADS,), ((0, 4),), -0.2, 0.2)), 0.02, 2.0)
    skip_gains = jnp.clip(0.5 + 1.0 * jax.random.uniform(arg_keys[5], (HEADS,), jnp.float32) ** shard_levels(arg_keys[5], (HEADS,), ((0, 4),), -0.2, 0.2), 0.5, 1.5)
    doc_lengths = ragged_sizes(arg_keys[6], NDOCS, TOKENS, DOC_SPAN * TOK_DEV, 2).astype(jnp.int32)
    out_grad = centred(arg_keys[7], (TOKENS, HEADS * HEAD_SIZE), 1.0, 6.0, ((0, 64), (1, 4)), jnp.float32)
    return {"values": values, "input_map": input_map, "output_map": output_map, "step_sizes": step_sizes, "decay_rates": decay_rates, "skip_gains": skip_gains, "doc_lengths": doc_lengths, "out_grad": out_grad}


highest = lax.Precision.HIGHEST


def edge_decays(log_decay, restart):
    running = jnp.cumsum(log_decay, axis=1)
    resets_seen = jnp.cumsum(restart)
    inward = jnp.where(resets_seen[None, :] == 0, jnp.exp(running), 0.0)
    outward = jnp.where(resets_seen[None, :] == resets_seen[-1], jnp.exp(running[:, -1:] - running), 0.0)
    whole_decay = jnp.where(resets_seen[-1] == 0, jnp.exp(running[:, -1]), 0.0)
    return running, resets_seen, inward, outward, whole_decay


def group_pass(values, bmat, cmat, steps, rates, skips, restart, grad_y):
    length, head_count, head_width = values.shape
    blocks = length // GROUP
    log_decay = -rates[:, None] * steps

    def blocked(array):
        return array.reshape((blocks, GROUP) + array.shape[1:])

    def blocked_heads(array):
        return jnp.transpose(array.reshape(head_count, blocks, GROUP), (1, 0, 2))

    grouped = (blocked(values), blocked(grad_y), blocked(bmat), blocked(cmat), blocked_heads(steps), blocked_heads(log_decay), blocked(restart))
    causal = jnp.arange(GROUP)[:, None] >= jnp.arange(GROUP)[None, :]

    def forward(carry_state, item):
        piece_x, piece_g, piece_b, piece_c, piece_dt, piece_log, piece_reset = item
        running, resets_seen, inward, outward, whole_decay = edge_decays(piece_log, piece_reset)
        visible = causal & (resets_seen[:, None] == resets_seen[None, :])
        inner = jnp.where(visible[None], jnp.exp(jnp.minimum(running[:, :, None] - running[:, None, :], 0.0)), 0.0)
        scaled = piece_x * piece_dt.T[:, :, None]
        scores = jnp.dot(piece_c, piece_b.T, precision=highest)
        mixing = inner * scores[None]
        entering = inward.T[:, :, None]
        result = jnp.einsum('hts,shp->thp', mixing, scaled, precision=highest)
        result = result + entering * jnp.einsum('tn,hpn->thp', piece_c, carry_state, precision=highest)
        result = result + skips[None, :, None] * piece_x
        products = jnp.einsum('thp,shp->hts', piece_g, piece_x, precision=highest)
        weight = inner * products * piece_dt[:, None, :]
        grad_x = jnp.einsum('hts,thp->shp', mixing, piece_g, precision=highest) * piece_dt.T[:, :, None]
        grad_x = grad_x + skips[None, :, None] * piece_g
        grad_b = jnp.einsum('hts,tn->sn', weight, piece_c, precision=highest)
        grad_c = jnp.einsum('hts,sn->tn', weight, piece_b, precision=highest)
        grad_c = grad_c + jnp.einsum('hpn,thp->tn', carry_state, piece_g * entering, precision=highest)
        updated = whole_decay[:, None, None] * carry_state + jnp.einsum('shp,sn->hpn', scaled * outward.T[:, :, None], piece_b, precision=highest)
        return updated, (result, grad_x, grad_b, grad_c, inward, outward, whole_decay)

    zeros_state = jnp.zeros((head_count, head_width, bmat.shape[1]), jnp.float32)
    end_state, outs = lax.scan(forward, zeros_state, grouped)
    result, grad_x, grad_b, grad_c, inwards, outwards, wholes = outs

    def backward(carry_grad, item):
        piece_x, piece_g, piece_b, piece_c, piece_dt, inward, outward, whole_decay = item
        factor = (piece_dt * outward).T[:, :, None]
        extra_x = factor * jnp.einsum('hpn,sn->shp', carry_grad, piece_b, precision=highest)
        extra_b = jnp.einsum('hpn,shp->sn', carry_grad, piece_x * factor, precision=highest)
        earlier_grad = whole_decay[:, None, None] * carry_grad + jnp.einsum('thp,tn->hpn', piece_g * inward.T[:, :, None], piece_c, precision=highest)
        return earlier_grad, (extra_x, extra_b)

    start_grad, (extra_x, extra_b) = lax.scan(backward, zeros_state, (grouped[0], grouped[1], grouped[2], grouped[3], grouped[4], inwards, outwards, wholes), reverse=True)
    result = result.reshape(length, head_count, head_width)
    grad_x = (grad_x + extra_x).reshape(length, head_count, head_width)
    grad_b = (grad_b + extra_b).reshape(length, -1)
    grad_c = grad_c.reshape(length, -1)
    return result, grad_x, grad_b, grad_c, end_state, start_grad


def reference(values, input_map, output_map, step_sizes, decay_rates, skip_gains, doc_lengths, out_grad):
    starts = (jnp.cumsum(doc_lengths) - doc_lengths).astype(jnp.int32)
    restart = jnp.zeros((TOKENS,), jnp.float32).at[starts].set(1.0)
    shaped_x = values.reshape(TOKENS, HEADS, HEAD_SIZE)
    shaped_g = out_grad.reshape(TOKENS, HEADS, HEAD_SIZE)
    result, grad_x, grad_b, grad_c, end_state, start_grad = group_pass(shaped_x, input_map, output_map, step_sizes, decay_rates, skip_gains, restart, shaped_g)
    return (result.reshape(TOKENS, -1).astype(jnp.bfloat16), grad_x.reshape(TOKENS, -1).astype(jnp.bfloat16), grad_b, grad_c)
```

```python
import functools

import jax
import jax.numpy as jnp
from jax import lax
from jax.experimental import pallas as pl
from jax.experimental.pallas import tpu as pltpu
from jax.sharding import PartitionSpec as P

HEAD_SIZE = 64
STATE = 128
F32 = jnp.float32
BF16 = jnp.bfloat16
INTERPRET = False

NN = (((1,), (0,)), ((), ()))
NT = (((1,), (1,)), ((), ()))
TN = (((0,), (0,)), ((), ()))


def exact(a, b, dims):
    return lax.dot_general(
        a, b, dims, precision=lax.Precision.HIGHEST, preferred_element_type=F32
    )


def halves(a):
    high = a.astype(BF16)
    return high, (a - high.astype(F32)).astype(BF16)


def dot3(a, b, dims):
    (ah, al), (bh, bl) = a, b
    one = functools.partial(lax.dot_general, dimension_numbers=dims, preferred_element_type=F32)
    return one(ah, bh) + (one(ah, bl) + one(al, bh))


def lanes_of(cols, pair, rows):
    lane = lax.broadcasted_iota(jnp.int32, (rows, 128), 1)
    left = jnp.broadcast_to(cols[:, 2 * pair : 2 * pair + 1], (rows, 128))
    right = jnp.broadcast_to(cols[:, 2 * pair + 1 : 2 * pair + 2], (rows, 128))
    return jnp.where(lane < HEAD_SIZE, left, right)


def call(kernel, outs, args, scalars=0, flops=0, name=None):
    specs = [pl.BlockSpec(memory_space=pltpu.SMEM)] * scalars
    specs += [pl.BlockSpec(memory_space=pltpu.VMEM)] * (len(args) - scalars)
    moved = sum(a.size * a.dtype.itemsize for a in list(args) + list(outs))
    return pl.pallas_call(
        kernel,
        out_shape=tuple(outs),
        in_specs=specs,
        out_specs=tuple(pl.BlockSpec(memory_space=pltpu.VMEM) for _ in outs),
        cost_estimate=pl.CostEstimate(flops=flops, bytes_accessed=moved, transcendentals=0),
        interpret=INTERPRET,
        name=name,
    )(*args)


def prepare(
    place, rates, lens, steps, x, g, bmat, cmat, pack, xs_ref, ge_ref, er_ref, de_ref, mask, row, end
):
    heads, length = steps.shape
    docs = lens.shape[1]
    first = place[0].astype(F32)
    lengths = jnp.broadcast_to(lens[...].astype(F32), (8, docs))
    up = lax.broadcasted_iota(jnp.int32, (docs, docs), 0)
    across = lax.broadcasted_iota(jnp.int32, (docs, docs), 1)
    start_row = exact(lengths, (up < across).astype(F32), NN)[0:1, :]
    start_col = exact((across < up).astype(F32), lengths, NT)[:, 0:1]
    at_col = first + lax.broadcasted_iota(jnp.int32, (length, docs), 0).astype(F32)
    at_row = first + lax.broadcasted_iota(jnp.int32, (docs, length), 1).astype(F32)
    doc_col = jnp.sum((start_row <= at_col).astype(F32), axis=1, keepdims=True)
    doc_row = jnp.sum((start_col <= at_row).astype(F32), axis=0, keepdims=True)
    before = jnp.sum((start_row < first).astype(F32), axis=1, keepdims=True)
    last = jnp.sum((start_row <= first + (length - 1)).astype(F32), axis=1, keepdims=True)
    inside = (doc_col == before).astype(F32)
    onward = (doc_col == last).astype(F32)

    head_at = lax.broadcasted_iota(jnp.int32, (heads, length), 0)
    rate = jnp.zeros((heads, length), F32)
    for h in range(heads):
        rate = jnp.where(head_at == h, rates[h], rate)
    dt = steps[...]
    log_decay = -rate * dt
    t_at = lax.broadcasted_iota(jnp.int32, (length, length), 0)
    s_at = lax.broadcasted_iota(jnp.int32, (length, length), 1)
    running = exact((s_at <= t_at).astype(F32), log_decay, NT)
    dt_col = exact((s_at == t_at).astype(F32), dt, NT)
    er = jnp.exp(running)
    de = dt_col * jnp.exp(-running)
    er_ref[...] = er
    de_ref[...] = de
    ended = jnp.exp(jnp.broadcast_to(jnp.sum(log_decay, axis=1, keepdims=True), (heads, 128)))
    end[...] = ended
    whole = ended * (before == last).astype(F32)

    lane = lax.broadcasted_iota(jnp.int32, (length, 128), 1)
    mask[...] = jnp.where(lane == 0, inside, jnp.where(lane == 1, onward, doc_col))
    row[...] = jnp.broadcast_to(doc_row, (8, length))

    b_out = halves(bmat[...] * onward)
    c_in = halves(cmat[...] * inside)
    for j in range(heads // 2):
        part = slice(128 * j, 128 * j + 128)
        scaled = x[:, part] * lanes_of(de, j, length)
        xs_ref[:, part] = scaled
        state = dot3(halves(scaled), b_out, TN)
        grown = g[:, part] * lanes_of(er, j, length)
        ge_ref[:, part] = grown
        grad = dot3(halves(grown), c_in, TN)
        for k in range(2):
            h, rows = 2 * j + k, slice(64 * k, 64 * k + 64)
            pack[h, 0:64, :] = state[rows, :] * ended[h : h + 1, :]
            pack[h, 64:128, :] = grad[rows, :]
            pack[h, 128:136, :] = jnp.broadcast_to(whole[h : h + 1, :], (8, 128))


def chip_states(place, mine, other, fwd, bwd, decay):
    core = place[1]
    half = fwd.shape[0]
    for k in range(half):
        h = core * half + k
        a, b = mine[h], other[h]
        early = jnp.where(core == 0, a, b)
        late = jnp.where(core == 0, b, a)
        d_early, d_late = early[128:129, :], late[128:129, :]
        fwd[k] = late[0:64, :] + d_late * early[0:64, :]
        bwd[k] = early[64:128, :] + d_early * late[64:128, :]
        decay[k] = jnp.broadcast_to(d_early * d_late, (8, 128))


def two_chips(fwd, bwd, decay, fwd_in, bwd_in, fwd_out, bwd_out):
    for k in range(fwd.shape[0]):
        d = decay[k][0:1, :]
        fwd_out[k] = fwd[k] + d * fwd_in[k]
        bwd_out[k] = bwd[k] + d * bwd_in[k]


def local(bmat, cmat, xs, ge, mask, row, y0, gx0, gb0, gc0):
    length = bmat.shape[0]
    t_at = lax.broadcasted_iota(jnp.int32, (length, length), 0)
    s_at = lax.broadcasted_iota(jnp.int32, (length, length), 1)
    seen = (mask[:, 2:3] == row[0:1, :]) & (s_at <= t_at)
    b2, c2, x2, g2 = halves(bmat[...]), halves(cmat[...]), halves(xs[...]), halves(ge[...])
    scores = halves(jnp.where(seen, dot3(c2, b2, NT), 0.0))
    y0[...] = dot3(scores, x2, NN)
    gx0[...] = dot3(scores, g2, TN)
    weight = halves(jnp.where(seen, dot3(g2, x2, NT), 0.0))
    gb0[...] = dot3(weight, c2, TN)
    gc0[...] = dot3(weight, b2, NN)


def finish_maps(
    place, other, f_own, f_far, b_own, b_far, end, xs, ge, mask, gb0, gc0, gb, gc, s_ref, a_ref
):
    core = place[1]
    heads = other.shape[0]
    half = heads // 2
    for h in range(heads):
        own = core == h // half
        k = h % half
        fwd = jnp.where(own, f_own[k], f_far[k])
        bwd = jnp.where(own, b_own[k], b_far[k])
        d = other[h, 128:129, :]
        state = jnp.where(core == 1, other[h, 0:64, :] + d * fwd, fwd)
        after = jnp.where(core == 0, other[h, 64:128, :] + d * bwd, bwd)
        s_ref[64 * h : 64 * h + 64, :] = state
        a_ref[64 * h : 64 * h + 64, :] = after * end[h : h + 1, :]
    state, after = halves(s_ref[...]), halves(a_ref[...])
    gc[...] = gc0[...] + mask[:, 0:1] * dot3(halves(ge[...]), state, NN)
    gb[...] = gb0[...] + mask[:, 1:2] * dot3(halves(xs[...]), after, NN)


def finish_values(skips, x, g, bmat, cmat, er, de, mask, s_ref, a_ref, y0, gx0, y, gx):
    length = bmat.shape[0]
    c_in = halves(cmat[...] * mask[:, 0:1])
    b_out = halves(bmat[...] * mask[:, 1:2])
    er_cols, de_cols = er[...], de[...]
    lane = lax.broadcasted_iota(jnp.int32, (1, 128), 1)
    for j in range(x.shape[1] // 128):
        part = slice(128 * j, 128 * j + 128)
        skip = jnp.where(lane < HEAD_SIZE, skips[2 * j], skips[2 * j + 1])
        far = dot3(c_in, halves(s_ref[part, :]), NT)
        y[:, part] = (
            lanes_of(er_cols, j, length) * (y0[:, part] + far) + skip * x[:, part]
        ).astype(BF16)
        far = dot3(b_out, halves(a_ref[part, :]), NT)
        gx[:, part] = (
            lanes_of(de_cols, j, length) * (gx0[:, part] + far) + skip * g[:, part]
        ).astype(BF16)


def body(values, input_map, output_map, step_sizes, decay_rates, skip_gains, doc_lengths, out_grad):
    length, width = values.shape
    heads = width // HEAD_SIZE
    half = heads // 2
    shape = jax.ShapeDtypeStruct
    index = lax.axis_index("seq")
    place = jnp.stack([index * length, index % 2]).astype(jnp.int32)
    count = lax.axis_size("seq")
    swap = [(i, i ^ 1) for i in range(count)]
    ahead = [(i, i + 2) for i in range(count - 2)]
    back = [(i + 2, i) for i in range(count - 2)]

    pack, xs, ge, er, de, mask, row, end = call(
        prepare,
        [
            shape((heads, 136, STATE), F32),
            shape((length, width), F32),
            shape((length, width), F32),
            shape((length, heads), F32),
            shape((length, heads), F32),
            shape((length, 128), F32),
            shape((8, length), F32),
            shape((heads, 128), F32),
        ],
        (
            place,
            decay_rates,
            doc_lengths.reshape(1, -1),
            step_sizes,
            values,
            out_grad,
            input_map,
            output_map,
        ),
        scalars=2,
        flops=12 * length * width * STATE,
        name="prepare",
    )
    other = lax.ppermute(pack, "seq", swap)
    y0, gx0, gb0, gc0 = call(
        local,
        [
            shape((length, width), F32),
            shape((length, width), F32),
            shape((length, STATE), F32),
            shape((length, STATE), F32),
        ],
        (input_map, output_map, xs, ge, mask, row),
        flops=18 * length * width * length,
        name="local",
    )
    states = shape((half, HEAD_SIZE, STATE), F32)
    fwd, bwd, decay = call(
        chip_states,
        [states, states, shape((half, 8, STATE), F32)],
        (place, pack, other),
        scalars=1,
        name="chip_states",
    )
    fwd_in = lax.ppermute(fwd, "seq", ahead)
    bwd_in = lax.ppermute(bwd, "seq", back)
    fwd, bwd = call(two_chips, [states, states], (fwd, bwd, decay, fwd_in, bwd_in), name="two_chips")
    f_own = lax.ppermute(fwd, "seq", ahead)
    b_own = lax.ppermute(bwd, "seq", back)
    f_far = lax.ppermute(f_own, "seq", swap)
    b_far = lax.ppermute(b_own, "seq", swap)
    gb, gc, state, after = call(
        finish_maps,
        [
            shape((length, STATE), F32),
            shape((length, STATE), F32),
            shape((width, STATE), F32),
            shape((width, STATE), F32),
        ],
        (place, other, f_own, f_far, b_own, b_far, end, xs, ge, mask, gb0, gc0),
        scalars=1,
        flops=12 * length * width * STATE,
        name="finish_maps",
    )
    near = [(0, 1), (1, 0), (2, 3), (3, 2)]
    cross = [(0, 3), (3, 0), (1, 2), (2, 1)]
    gb = gb + lax.ppermute(gb, "head", near)
    gc = gc + lax.ppermute(gc, "head", cross)
    y, gx = call(
        finish_values,
        [shape((length, width), BF16), shape((length, width), BF16)],
        (
            skip_gains,
            values,
            out_grad,
            input_map,
            output_map,
            er,
            de,
            mask,
            state,
            after,
            y0,
            gx0,
        ),
        scalars=1,
        flops=12 * length * width * STATE,
        name="finish_values",
    )
    gb = gb + lax.ppermute(gb, "head", cross)
    gc = gc + lax.ppermute(gc, "head", near)
    return y, gx, gb, gc


def solution(mesh):
    placed = (
        P("seq", "head"),
        P("seq", None),
        P("seq", None),
        P("head", "seq"),
        P("head"),
        P("head"),
        P(),
        P("seq", "head"),
    )
    return jax.shard_map(
        body,
        mesh=mesh,
        in_specs=placed,
        out_specs=(P("seq", "head"), P("seq", "head"), P("seq", None), P("seq", None)),
        check_vma=False,
    )
```
